512 devices in a mesh: pack: 16 (over y, x), seq: 32 (over z, core).
Axes of the slice: x: 4, y: 4, z: 16, core: 2. Of those that a mesh axis runs over, the one named last changes fastest.
Arguments:
- queries: bfloat16 [65536, 2048], P(('pack', 'seq')), parts along dimension 0, may hold values from -48 to 48
- token_key_heads: bfloat16 [65536, 256], P(('pack', 'seq')), parts along dimension 0, may hold values from -6 to 6
- token_value_heads: bfloat16 [65536, 256], P(('pack', 'seq')), parts along dimension 0, may hold values from -6 to 6
- residual: bfloat16 [65536, 1024], P(('pack', 'seq')), parts along dimension 0, may hold values from -40 to 40
- out_weight: bfloat16 [2048, 1024], P('seq'), may hold values from -0.125 to 0.125
- norm_gain: bfloat16 [1024], replicated, may hold values from 0.5 to 1.5
- w_gate: bfloat16 [32, 1024, 384], P('seq'), may hold values from -0.1875 to 0.1875
- w_up: bfloat16 [32, 1024, 384], P('seq'), may hold values from -0.1875 to 0.1875
- w_down: bfloat16 [32, 384, 1024], P('seq'), may hold values from -0.3125 to 0.3125
- expert_ids: int32 [65536, 8], P(('pack', 'seq')), parts along dimension 0, may hold values from 0 to 31, all different within a row; in each aligned block of 128 rows (0 to 127, 128 to 255, ...) at most 48 rows name the same one
- gate_weights: float32 [65536, 8], P(('pack', 'seq')), parts along dimension 0, may hold values from 0.05 to 0.3
- doc_of_block: int32 [512], P('pack'), parts along dimension 0, may hold values from 0 to 7, never falling along the last dimension, each value on 1 to 8 neighbouring positions
Outputs:
- attention: bfloat16 [65536, 2048], P(('pack', 'seq')), parts along dimension 0
- hidden_out: bfloat16 [65536, 1024], P(('pack', 'seq')), parts along dimension 0
- expert_mix: bfloat16 [65536, 1024], P(('pack', 'seq')), parts along dimension 0
The draws below stay inside these ranges and needn't reach their ends.
There are 16 independent parts, one for each index of `pack`. The reference program is written for one: setup_inputs(seed, part) draws one part's arguments, and reference() takes and returns one part's arrays. A program takes and returns all parts, laid end to end along the dimension named above; an argument that names none is the same for every part. Nothing has to cross between parts.
Inputs may be any that keep to these rules, and one draw needn't show every extreme that they name: `expert_ids`: each row names 8 different experts; within the rows of one block no expert is named more than 48 times, and in every draw some expert is named exactly 48 times by the rows of some block. `doc_of_block`: never falls from block to block; each document covers 1 to 8 blocks, one exactly 8.
All inputs are finite; a program needn't handle non-finite values.
Results may differ from the reference program's by a relative error of at most 0.015.
Values may be sent and summed in bfloat16 or wider, within the bound.
A program may use at most 64 MiB of HBM per device.

```python
import math
import jax
import jax.numpy as jnp
import numpy as np
from jax import lax

D = 1024
FF = 384
QUERY_HEADS = 16
KEY_VALUE_HEADS = 2
HEAD_SIZE = 128
TOP = 8
TOK_DEV = 128
SLAB_TOKENS = 4096
EXPERTS = 32
SLOT = 48
MOST_BLK = 8
DOCS = 8
N_SEQ = 32


def query_key_pair(key):
    base_key = jax.random.fold_in(key, 7103)
    query_key, head_random_key = jax.random.split(base_key, 2)
    query_random_draw = jnp.clip(jax.random.normal(query_key, (SLAB_TOKENS, QUERY_HEADS, HEAD_SIZE), jnp.float32), -6.0, 6.0)
    key_random_draw = jnp.clip(jax.random.normal(head_random_key, (SLAB_TOKENS, KEY_VALUE_HEADS, HEAD_SIZE), jnp.float32), -6.0, 6.0)
    return (query_random_draw.reshape(SLAB_TOKENS, QUERY_HEADS * HEAD_SIZE), key_random_draw.reshape(SLAB_TOKENS, KEY_VALUE_HEADS * HEAD_SIZE))


def draw_queries(key, part):
    return query_key_pair(key)[0].astype(jnp.bfloat16)


def draw_token_key_heads(key, part):
    return query_key_pair(key)[1].astype(jnp.bfloat16)


def draw_residual(key, part):
    base_key = jax.random.fold_in(key, 5081)
    row_key, col_key, jitter_key = jax.random.split(base_key, 3)
    row_scale = jnp.exp(jax.random.uniform(row_key, (SLAB_TOKENS, 1), jnp.float32, math.log(0.3), math.log(3.0)))
    col_scale = jnp.exp(jax.random.uniform(col_key, (1, D), jnp.float32, math.log(0.3), math.log(3.0)))
    jitter = jnp.clip(jax.random.normal(jitter_key, (SLAB_TOKENS, D), jnp.float32), -4.0, 4.0)
    return (jitter * row_scale * col_scale).astype(jnp.bfloat16)


def steps_of(rng, shape, cuts, smallest, top_value):
    gain = 1.0
    for axis_at, shards_of in cuts:
        draws = jax.random.uniform(jax.random.fold_in(jax.random.fold_in(rng, 6), axis_at), (shards_of,), jnp.float32, smallest / len(cuts), top_value / len(cuts))
        gain = gain * jnp.repeat(jnp.exp(draws), shape[axis_at] // shards_of).reshape((-1,) + (1,) * (len(shape) - 1 - axis_at))
    return gain


def length_profile(count, total, reach, skew):
    weights = [(1 << 20) // math.isqrt(rank ** skew) + 1 for rank in range(2, count + 1)]
    spare, holding = total - reach - (count - 1), [1] * (count - 1)
    while spare > 0:
        free = [i for i in range(count - 1) if holding[i] < reach]
        whole, budget = sum([weights[i] for i in free]), spare
        for i in free:
            extra = min(reach - holding[i], max(1, budget * weights[i] // whole), spare)
            holding[i] = holding[i] + extra
            spare = spare - extra
    return np.array([reach] + holding)


def uneven(key, count, total, most, skew):
    if count == 2:
        one = jax.random.randint(key, (), max(1, total - most), min(most, total - 1) + 1)
        return jnp.stack([one, total - one])
    lengths = jnp.asarray(length_profile(count, total, most, skew), jnp.int32)
    couples = (count - 1) // 2
    source_of, receiver = lengths[1:1 + 2 * couples:2], lengths[2:2 + 2 * couples:2]
    margin = jnp.minimum(source_of - 1, most - receiver)
    moved = jax.random.randint(jax.random.fold_in(key, 1), (couples,), 0, 1 << 20) % (margin + 1)
    lengths = lengths.at[1:1 + 2 * couples:2].set(source_of - moved).at[2:2 + 2 * couples:2].set(receiver + moved)
    return lengths[jax.random.permutation(jax.random.fold_in(key, 2), count)]


def assign_block(key, own, number, rows, amount, top, reach, skew):
    ranking = jax.random.permutation(key, amount)
    packed, ordinary = shares(amount, rows * top, reach, skew, True), shares(amount, rows * top, reach, skew, False)
    places = jnp.arange(amount)

    def named(sizes, offset_by):
        used = int((sizes > 0).sum())
        fixed = max(1, used // 4)
        moved = fixed + (places - fixed + offset_by * (used - fixed)) % max(1, amount - fixed)
        return jnp.zeros((amount,), jnp.int32).at[ranking[jnp.where(places < fixed, places, moved)]].set(jnp.asarray(sizes, jnp.int32))

    sizes = jnp.where(number % 4 == 0, named(packed, number // 4), named(ordinary, number - number // 4 - 1))
    mixed = jax.random.permutation(jax.random.fold_in(own, 3), amount)
    donor, receiver = mixed[0:amount // 2 * 2:2], mixed[1:amount // 2 * 2:2]
    margin = jnp.minimum(sizes[donor] - 1, reach - sizes[receiver]) // 2
    margin = jnp.where((donor == ranking[0]) | (receiver == ranking[0]) | (sizes[receiver] == 0), 0, jnp.maximum(margin, 0))
    moved = jax.random.randint(jax.random.fold_in(own, 4), (amount // 2,), 0, 1 << 20) % (margin + 1)
    sizes = sizes.at[donor].add(-moved).at[receiver].add(moved)
    members = jnp.searchsorted(jnp.cumsum(sizes), jnp.arange(rows * top), side="right").astype(jnp.int32)
    table = members.reshape(top, rows).T
    table = table[jax.random.permutation(jax.random.fold_in(own, 1), rows)]
    offset_by = jax.random.randint(jax.random.fold_in(own, 2), (rows, 1), 0, top)
    return jnp.take_along_axis(table, (jnp.arange(top)[None, :] + offset_by) % top, axis=1)


def shares(number_of, total, reach, lean, full):
    portions = [(1 << 20) // math.isqrt(grade ** lean) + 1 for grade in range(1, number_of + 1)]
    largest = reach if full else min(reach, max(-(-total // number_of), total * portions[0] // sum(portions)))
    least = 1 if total - largest >= number_of - 1 else 0
    holding, surplus = [largest] + [least] * (number_of - 1), total - largest - least * (number_of - 1)
    while surplus > 0:
        candidates = [i for i in range(1, number_of) if holding[i] < largest] or [i for i in range(1, number_of) if holding[i] < reach]
        pool, left = sum([portions[i] for i in candidates]), surplus
        for i in candidates:
            extra = min(reach - holding[i], max(1, left * portions[i] // pool), surplus)
            holding[i] = holding[i] + extra
            surplus = surplus - extra
    return np.array(holding)


def noise(rng, extent, width, reach, pieces=(), kind=jnp.bfloat16):
    entries = width * jax.random.normal(rng, extent, jnp.float32)
    if pieces:
        entries = entries * steps_of(rng, extent, pieces, -0.22, 0.18)
    return jnp.clip(entries, -reach, reach).astype(kind)


def setup_inputs(seed: int = 0, part: int = 0) -> dict:
    seeds = jax.random.split(jax.random.key(seed), 13)
    part_keys = jax.random.split(jax.random.fold_in(seeds[12], part), 13)
    queries = draw_queries(jax.random.fold_in(jax.random.fold_in(seeds[12], part), 71), part)
    token_key_heads = draw_token_key_heads(jax.random.fold_in(jax.random.fold_in(seeds[12], part), 71), part)
    token_value_heads = noise(part_keys[2], (SLAB_TOKENS, KEY_VALUE_HEADS * HEAD_SIZE), 1.0, 6.0, ((0, 32),))
    residual = draw_residual(jax.random.fold_in(jax.random.fold_in(seeds[12], part), 71), part)
    out_weight = noise(seeds[4], (QUERY_HEADS * HEAD_SIZE, D), (QUERY_HEADS * HEAD_SIZE) ** -0.5, 0.125, ((0, 32),))
    norm_gain = jnp.clip(1.0 + 0.1 * jax.random.normal(seeds[5], (D,), jnp.float32), 0.5, 1.5).astype(jnp.bfloat16)
    w_gate = noise(seeds[6], (EXPERTS, D, FF), D ** -0.5, 0.1875, ((0, 32),))
    w_up = noise(seeds[7], (EXPERTS, D, FF), D ** -0.5, 0.1875, ((0, 32),))
    w_down = noise(seeds[8], (EXPERTS, FF, D), FF ** -0.5, 0.3125, ((0, 32),))
    expert_ids_keys = jax.random.split(jax.random.fold_in(part_keys[9], 1), SLAB_TOKENS // TOK_DEV)
    expert_ids_turns = jax.random.permutation(jax.random.fold_in(part_keys[9], 3), SLAB_TOKENS // TOK_DEV)
    expert_ids = jax.vmap(lambda own, number: assign_block(jax.random.fold_in(part_keys[9], 2), own, number, TOK_DEV, EXPERTS, TOP, SLOT, 2))(expert_ids_keys, expert_ids_turns).reshape((SLAB_TOKENS, TOP))
    gate_weights = jnp.clip(0.05 + 0.25 * jax.random.uniform(part_keys[10], (SLAB_TOKENS, TOP), jnp.float32) ** steps_of(part_keys[10], (SLAB_TOKENS, TOP), ((0, 32),), -0.2, 0.2), 0.05, 0.3)
    doc_of_block = jnp.searchsorted(jnp.cumsum(uneven(part_keys[11], DOCS, N_SEQ, MOST_BLK, 0)), jnp.arange(N_SEQ), side="right").astype(jnp.int32)
    return dict(queries=queries, token_key_heads=token_key_heads, token_value_heads=token_value_heads, residual=residual, out_weight=out_weight, norm_gain=norm_gain, w_gate=w_gate, w_up=w_up, w_down=w_down, expert_ids=expert_ids, gate_weights=gate_weights, doc_of_block=doc_of_block)


def reference(queries, token_key_heads, token_value_heads, residual, out_weight, norm_gain, w_gate, w_up, w_down, expert_ids, gate_weights, doc_of_block):
    heads_per_group = QUERY_HEADS // KEY_VALUE_HEADS
    query_every_head = queries.reshape(SLAB_TOKENS, KEY_VALUE_HEADS, heads_per_group, HEAD_SIZE).astype(jnp.float32)
    key_every_head = token_key_heads.reshape(SLAB_TOKENS, KEY_VALUE_HEADS, HEAD_SIZE).astype(jnp.float32)
    value_every_head = token_value_heads.reshape(SLAB_TOKENS, KEY_VALUE_HEADS, HEAD_SIZE).astype(jnp.float32)
    key_pos = jnp.arange(SLAB_TOKENS, dtype=jnp.int32)
    key_block = key_pos // TOK_DEV
    key_doc = doc_of_block[key_block]
    factor = 1.0 / HEAD_SIZE ** 0.5

    def attend_block(block):
        query_block = lax.dynamic_slice_in_dim(query_every_head, (block * TOK_DEV).astype(jnp.int32), TOK_DEV, 0)
        query_pos = block * TOK_DEV + jnp.arange(TOK_DEV, dtype=jnp.int32)
        allowed = (key_block <= block) & ((key_doc == doc_of_block[block]) | (key_block == 0))
        visible = allowed[None, :] & (key_pos[None, :] <= query_pos[:, None])
        scores = jnp.einsum('tkgd,skd->kgts', query_block, key_every_head) * factor
        scores = jnp.where(visible, scores, -1e+30)
        top_score = lax.optimization_barrier(jnp.max(scores, axis=-1, keepdims=True))
        terms = jnp.where(visible, jnp.exp(scores - top_score), 0.0)
        denom = lax.optimization_barrier(jnp.sum(terms, axis=-1))
        probs = lax.optimization_barrier(terms.astype(jnp.bfloat16)).astype(jnp.float32)
        summed = jnp.einsum('kgts,skd->tkgd', probs, value_every_head)
        result = summed / jnp.transpose(denom, (2, 0, 1))[..., None]
        return result.reshape(TOK_DEV, QUERY_HEADS * HEAD_SIZE).astype(jnp.bfloat16)
    attention = lax.map(attend_block, jnp.arange(N_SEQ, dtype=jnp.int32)).reshape(SLAB_TOKENS, QUERY_HEADS * HEAD_SIZE)
    hidden_state = residual.astype(jnp.float32) + jnp.dot(attention, out_weight, preferred_element_type=jnp.float32)
    mean_square = lax.optimization_barrier(jnp.mean(hidden_state * hidden_state, axis=-1, keepdims=True))
    normed = (hidden_state * lax.rsqrt(mean_square + 1e-06) * norm_gain.astype(jnp.float32)).astype(jnp.bfloat16)

    def one_expert(running, expert):
        gate_part = jnp.dot(normed, w_gate[expert], preferred_element_type=jnp.float32)
        up_part = jnp.dot(normed, w_up[expert], preferred_element_type=jnp.float32)
        activated = (jax.nn.silu(gate_part) * up_part).astype(jnp.bfloat16)
        produced = jnp.dot(activated, w_down[expert], preferred_element_type=jnp.float32).astype(jnp.bfloat16)
        weight = lax.optimization_barrier(jnp.sum(jnp.where(expert_ids == expert, gate_weights, 0.0), axis=-1))
        return (running + weight[:, None] * produced.astype(jnp.float32), None)
    expert_mix, _ = lax.scan(one_expert, jnp.zeros((SLAB_TOKENS, D), jnp.float32), jnp.arange(EXPERTS, dtype=jnp.int32))
    return (attention, hidden_state.astype(jnp.bfloat16), expert_mix.astype(jnp.bfloat16))
```

```python
import functools

import jax
import jax.numpy as jnp
from jax import lax
from jax.experimental import pallas as pl
from jax.experimental.pallas import tpu as pltpu
from jax.sharding import PartitionSpec as P

QUERY_HEADS = 16
KEY_VALUE_HEADS = 2
HEAD_SIZE = 128
TOP = 8
MESH = pl.DeviceIdType.MESH
HIDE = -1e30


def slab_kernel(
    chips,
    window,
    doc_ref,
    q_ref,
    k_ref,
    v_ref,
    res_ref,
    wo_ref,
    gain_ref,
    ids_ref,
    gw_ref,
    wg_hbm,
    wu_hbm,
    wd_hbm,
    attn_out,
    hid_out,
    mix_out,
    kv,
    qs,
    run_max,
    run_sum,
    oacc,
    heads,
    wfull,
    hidden,
    gate_send,
    gates,
    gate_cols,
    wgu,
    wd,
    xbuf,
    accbuf,
    contrib,
    own_part,
    kv_s,
    kv_r,
    sib_s,
    sib_r,
    first_s,
    first_r,
    w_s,
    w_r,
    wsib_s,
    wsib_r,
    g_s,
    g_r,
    load_s,
    ew_s,
    ew_r,
    x_s,
    x_r,
    a_s,
    a_r,
):
    me = lax.axis_index("seq")
    chip, core = me // 2, me % 2
    sib = chip * 2 + (1 - core)
    group = QUERY_HEADS // KEY_VALUE_HEADS
    tokens, width = res_ref.shape
    half = tokens // 2
    kvw = k_ref.shape[1]
    ff = wg_hbm.shape[2]
    hops = window // 2
    relay, first = window, window + 1

    def wrap(c):
        return lax.rem(c + 4 * chips, chips)

    def at(c):
        return wrap(c) * 2 + core

    nxt, prv = at(chip + 1), at(chip - 1)

    def rcopy(src, dst, ssem, rsem, dev):
        return pltpu.make_async_remote_copy(
            src_ref=src,
            dst_ref=dst,
            send_sem=ssem,
            recv_sem=rsem,
            device_id={"seq": dev},
            device_id_type=MESH,
        )

    def kv_hop(t):
        return rcopy(kv.at[2 * t], kv.at[2 * t + 2], kv_s.at[t], kv_r.at[t], nxt)

    def kv_share(t):
        return rcopy(
            kv.at[2 * t], kv.at[2 * (t - core) + 1], sib_s.at[t - core], sib_r.at[t - core], sib
        )

    def kv_shared(t):
        return rcopy(kv.at[2 * t + 1], kv.at[2 * t + 1], sib_s.at[t], sib_r.at[t], sib)

    def w_chip(d, t):
        return wrap(chip - t) if d == 0 else wrap(chip + t)

    def w_hop(d, t):
        ref = wfull.at[w_chip(d, t) * 2 + core]
        return rcopy(ref, ref, w_s.at[d, t], w_r.at[d, t], nxt if d == 0 else prv)

    def w_arrived(d, t):
        ref = wfull.at[w_chip(d, t) * 2 + core]
        return rcopy(ref, ref, w_s.at[d, t - 1], w_r.at[d, t - 1], nxt if d == 0 else prv)

    def w_share(d, t):
        ref = wfull.at[w_chip(d, t) * 2 + core]
        return rcopy(ref, ref, wsib_s.at[d, t], wsib_r.at[d, t], sib)

    def w_shared(d, t):
        ref = wfull.at[w_chip(d, t) * 2 + (1 - core)]
        return rcopy(ref, ref, wsib_s.at[d, t], wsib_r.at[d, t], sib)

    def gate_copy(d):
        to = wrap(chip + d)
        return rcopy(gate_send.at[to], gates.at[chip], g_s.at[d], g_r.at[d], to * 2 + core)

    def gate_arrived(d):
        ref = gates.at[wrap(chip - d)]
        return rcopy(ref, ref, g_s.at[d], g_r.at[d], nxt)

    def first_copy(n, dev):
        return rcopy(kv.at[first], kv.at[first], first_s.at[n], first_r, dev)

    def cols(e):
        return pl.ds(pl.multiple_of(e * ff, 128), ff)

    def up_cols(e):
        return pl.ds(pl.multiple_of((2 + e) * ff, 128), ff)

    def rows(e):
        return pl.ds(pl.multiple_of(e * ff, 128), ff)

    weights = (
        (wg_hbm.at[0], wgu.at[:, cols(core)], wgu.at[:, cols(1 - core)]),
        (wu_hbm.at[0], wgu.at[:, up_cols(core)], wgu.at[:, up_cols(1 - core)]),
        (wd_hbm.at[0], wd.at[rows(core)], wd.at[rows(1 - core)]),
    )

    def x_hop(d, s):
        return rcopy(
            xbuf.at[d, s], xbuf.at[d, s + 1], x_s.at[d, s], x_r.at[d, s], nxt if d == 0 else prv
        )

    def a_hop(d, s):
        return rcopy(
            accbuf.at[d, s], accbuf.at[d, s + 1], a_s.at[d, s], a_r.at[d, s], nxt if d == 0 else prv
        )

    kv[0, :, :kvw] = k_ref[...]
    kv[0, :, kvw:] = v_ref[...]
    wfull[me] = wo_ref[...]
    barrier = pltpu.get_barrier_semaphore()

    def greet(d, carry):
        pl.semaphore_signal(
            barrier, inc=1, device_id={"seq": at(chip + d)}, device_id_type=MESH
        )
        return carry

    lax.fori_loop(1, chips, greet, 0)
    pl.semaphore_signal(barrier, inc=1, device_id={"seq": sib}, device_id_type=MESH)
    pl.semaphore_wait(barrier, chips)

    kv_hop(0).start()

    @pl.when(core == 0)
    def _():
        kv_share(0).start()

    w_hop(1, 0).start()

    reached = tuple(range(chips - 1, 4, -2))

    @pl.when(me == 0)
    def _():
        for n, c in enumerate(reached):
            rcopy(kv.at[0], kv.at[first], first_s.at[n], first_r, 2 * c).start()

    w_hop(0, 0).start()
    w_share(0, 0).start()

    @pl.when(chip < 4)
    def _():
        kv[first] = kv[0]

    for n, (src, mine, _) in enumerate(weights):
        pltpu.make_async_copy(src, mine, load_s.at[n]).start()

    lane = lax.broadcasted_iota(jnp.int32, (tokens, 128), 1)
    dense = jnp.zeros((tokens, 128), jnp.float32)
    for n in range(TOP):
        dense = dense + jnp.where(lane == ids_ref[:, n : n + 1], gw_ref[:, n : n + 1], 0.0)
    by_expert = dense.T
    for c in range(chips):
        gate_send[c] = by_expert[2 * c : 2 * c + 2]
    gates[chip] = gate_send[chip]

    def send_gates(d, carry):
        gate_copy(d).start()
        return carry

    lax.fori_loop(1, chips, send_gates, 0)

    for h in range(QUERY_HEADS):
        qs[h // group, (h % group) * tokens : (h % group + 1) * tokens, :] = q_ref[
            :, h * HEAD_SIZE : (h + 1) * HEAD_SIZE
        ]
    run_max[...] = jnp.full_like(run_max, HIDE)
    run_sum[...] = jnp.zeros_like(run_sum)
    oacc[...] = jnp.zeros_like(oacc)
    factor = 1.0 / HEAD_SIZE**0.5

    def attend(slot, seen):
        key_at = lax.broadcasted_iota(jnp.int32, (tokens, tokens), 0)
        query_at = lax.broadcasted_iota(jnp.int32, (tokens, tokens), 1)
        bias = jnp.where(seen, 0.0, HIDE).astype(jnp.float32)
        late = (key_at > query_at) & (slot == 0)
        tile = jnp.where(late, HIDE, bias)
        tile = jnp.concatenate([tile] * group, axis=1)
        for g in range(KEY_VALUE_HEADS):
            keys = kv[slot, :, g * HEAD_SIZE : (g + 1) * HEAD_SIZE]
            values = kv[slot, :, kvw + g * HEAD_SIZE : kvw + (g + 1) * HEAD_SIZE]
            s = lax.dot_general(
                keys, qs[g], (((1,), (1,)), ((), ())), preferred_element_type=jnp.float32
            )
            s = s * factor + tile
            old = run_max[g]
            new = jnp.maximum(old, jnp.max(s, axis=0, keepdims=True))
            p = jnp.exp(s - new)
            fade = jnp.exp(old - new)
            run_max[g] = new
            run_sum[g] = run_sum[g] * fade + jnp.sum(p, axis=0, keepdims=True)
            oacc[g] = oacc[g] * fade + lax.dot_general(
                values,
                p.astype(jnp.bfloat16),
                (((0,), (0,)), ((), ())),
                preferred_element_type=jnp.float32,
            )

    own_doc = doc_ref[me]

    def seen_of(slot):
        blk = me - slot
        doc = doc_ref[jnp.maximum(blk, 0)]
        return (blk == 0) | ((blk > 0) & (doc == own_doc))

    def w_step(t, down=True):
        if down:
            w_arrived(0, t).wait_recv()

            @pl.when(t < chips // 2 - 1)
            def _():
                w_hop(0, t).start()

            w_share(0, t).start()
        w_arrived(1, t).wait_recv()

        @pl.when(t < chips // 2)
        def _():
            w_hop(1, t).start()

        w_share(1, t).start()

    for n, (src, mine, _) in enumerate(weights):
        pltpu.make_async_copy(src, mine, load_s.at[n]).wait()
        rcopy(mine, mine, ew_s.at[n], ew_r.at[n], sib).start()

    attend(0, me >= 0)

    def window_step(t, carry):
        kv_hop(t - 1).wait_recv()

        @pl.when((t < hops - 1) | (core == 1))
        def _():
            kv_hop(t).start()

        kv_share(t).start()
        w_step(t)

        def both(n, inner):
            slot = 2 * t - n

            @pl.when(n == 1)
            def _():
                kv_shared(t - 1).wait_recv()

            attend(slot, seen_of(slot))
            return inner

        lax.fori_loop(0, 2, both, 0)

        @pl.when((t == 2) & (core == 0) & (chip >= 5) & (chip % 2 == 1))
        def _():
            first_copy(0, sib).wait_recv()
            first_copy(0, at(chip - 1)).start()
            first_copy(1, sib).start()

        @pl.when((t == 3) & (core == 0) & (chip >= 4) & (chip % 2 == 0))
        def _():
            first_copy(1, sib).wait_recv()
            first_copy(1, sib).start()

        return carry

    lax.fori_loop(1, hops, window_step, 0)

    @pl.when(core == 1)
    def _():
        kv_hop(hops - 1).wait_recv()
        kv_share(hops).start()

    w_step(hops)
    kv_shared(hops - 1).wait_recv()

    @pl.when((core == 1) & (chip >= 4))
    def _():
        first_copy(0, sib).wait_recv()

    def rest(n, carry):
        slot = window - 1 + 2 * n
        attend(slot, ((n == 0) & seen_of(window - 1)) | ((n == 1) & (me >= window)))
        return carry

    lax.fori_loop(0, 2, rest, 0)

    for g in range(KEY_VALUE_HEADS):
        done = oacc[g] / run_sum[g]
        for n in range(group):
            h = g * group + n
            one = done[:, n * tokens : (n + 1) * tokens].T.astype(jnp.bfloat16)
            attn_out[:, h * HEAD_SIZE : (h + 1) * HEAD_SIZE] = one
            heads[h] = one

    hidden[...] = res_ref[...].astype(jnp.float32)

    def project(c):
        part = wfull[pl.ds(2 * c, 2)].reshape(2 * wo_ref.shape[0], width)
        hidden[...] += jnp.dot(heads[c], part, preferred_element_type=jnp.float32)

    w_shared(0, 0).wait_recv()
    project(chip)

    def project_step(t, carry):
        @pl.when(t > hops)
        def _():
            w_step(t)

        w_shared(0, t).wait_recv()
        project(w_chip(0, t))
        w_shared(1, t).wait_recv()
        project(w_chip(1, t))
        return carry

    lax.fori_loop(1, chips // 2, project_step, 0)
    w_step(chips // 2, down=False)
    w_shared(1, chips // 2).wait_recv()
    project(w_chip(1, chips // 2))

    state = hidden[...]
    hid_out[...] = state.astype(jnp.bfloat16)
    mean_square = jnp.mean(state * state, axis=-1, keepdims=True)
    normed = (
        state * lax.rsqrt(mean_square + 1e-06) * gain_ref[...].astype(jnp.float32)
    ).astype(jnp.bfloat16)
    xbuf[0, 0] = normed[:half]
    xbuf[1, 0] = normed[half:]
    for d in range(2):
        x_hop(d, 0).start()

    def wait_gates(d, carry):
        gate_arrived(d).wait_recv()
        return carry

    lax.fori_loop(1, chips, wait_gates, 0)
    stacked = jnp.concatenate(
        [gates[c] for c in range(chips)]
        + [jnp.zeros((128 - 2 * chips, tokens), jnp.float32)],
        axis=0,
    )
    gate_cols[...] = stacked.T
    for n, (_, _, theirs) in enumerate(weights):
        rcopy(theirs, theirs, ew_s.at[n], ew_r.at[n], sib).wait_recv()

    def served(s):
        row = lax.broadcasted_iota(jnp.int32, (tokens, 128), 0)
        x = xbuf[:, s].reshape(tokens, width)
        both = jnp.dot(x, wgu[...], preferred_element_type=jnp.float32)
        home = jnp.where(row < half, wrap(chip - s), wrap(chip + s)) * 2
        parts = []
        for e in range(2):
            gate = jnp.sum(
                jnp.where(lane == home + e, gate_cols[...], 0.0), axis=1, keepdims=True
            )
            v = both[:, e * ff : (e + 1) * ff]
            u = both[:, (2 + e) * ff : (3 + e) * ff]
            parts.append((v / (1.0 + jnp.exp(-v)) * u * gate).astype(jnp.bfloat16))
        return jnp.dot(
            jnp.concatenate(parts, axis=1), wd[...], preferred_element_type=jnp.float32
        )

    own_part[...] = served(0)
    last = chips - 1

    def take_x(s):
        for d in range(2):
            x_hop(d, s - 1).wait_recv()

            @pl.when(s < last)
            def _():
                x_hop(d, s).start()

    take_x(1)
    contrib[...] = served(1)

    def ring_step(s, carry):
        @pl.when(s < last)
        def _():
            take_x(s + 1)

        @pl.when(s > 1)
        def _():
            for d in range(2):
                a_hop(d, s - 1).wait_recv()
                part = slice(d * half, (d + 1) * half)
                accbuf[d, s] = (contrib[part] + accbuf[d, s].astype(jnp.float32)).astype(
                    jnp.bfloat16
                )
                a_hop(d, s).start()

        @pl.when(s == 1)
        def _():
            for d in range(2):
                accbuf[d, s] = contrib[d * half : (d + 1) * half].astype(jnp.bfloat16)
                a_hop(d, s).start()

        @pl.when(s < last)
        def _():
            contrib[...] = served(s + 1)

        return carry

    lax.fori_loop(1, chips, ring_step, 0)
    for d in range(2):
        a_hop(d, last).wait_recv()
        part = slice(d * half, (d + 1) * half)
        mix_out[part] = (own_part[part] + accbuf[d, chips].astype(jnp.float32)).astype(
            jnp.bfloat16
        )

    for t in range(hops - 1):
        kv_hop(t).wait_send()

    @pl.when(core == 1)
    def _():
        kv_hop(hops - 1).wait_send()

    for t in range(hops):
        kv_shared(t).wait_send()

    @pl.when(me == 0)
    def _():
        for n in range(len(reached)):
            first_copy(n, sib).wait_send()

    @pl.when((core == 0) & (chip >= 4))
    def _():
        first_copy(1, sib).wait_send()

    @pl.when((core == 0) & (chip >= 5) & (chip % 2 == 1))
    def _():
        first_copy(0, sib).wait_send()

    def sent_w(t, carry):
        w_hop(0, t).wait_send()
        w_hop(1, t).wait_send()
        w_share(0, t).wait_send()
        w_share(1, t + 1).wait_send()
        return carry

    lax.fori_loop(0, chips // 2 - 1, sent_w, 0)
    w_hop(1, chips // 2 - 1).wait_send()
    w_share(0, chips // 2 - 1).wait_send()
    w_share(1, chips // 2).wait_send()

    def sent(s, carry):
        gate_copy(s).wait_send()
        for d in range(2):
            x_hop(d, s - 1).wait_send()
            a_hop(d, s).wait_send()
        return carry

    lax.fori_loop(1, chips, sent, 0)
    for n, (_, mine, _) in enumerate(weights):
        rcopy(mine, mine, ew_s.at[n], ew_r.at[n], sib).wait_send()


def shards(
    queries,
    token_key_heads,
    token_value_heads,
    residual,
    out_weight,
    norm_gain,
    w_gate,
    w_up,
    w_down,
    expert_ids,
    gate_weights,
    doc_of_block,
):
    blocks = lax.axis_size("seq")
    chips = blocks // 2
    tokens, width = residual.shape
    heads_width = queries.shape[1]
    kvw = token_key_heads.shape[1]
    ff = w_gate.shape[2]
    window = 8
    group_rows = tokens * QUERY_HEADS // KEY_VALUE_HEADS
    half = tokens // 2
    vmem = pl.BlockSpec(memory_space=pltpu.VMEM)
    hbm = pl.BlockSpec(memory_space=pl.ANY)
    dma = pltpu.SemaphoreType.DMA
    bf16, f32 = jnp.bfloat16, jnp.float32
    return pl.pallas_call(
        functools.partial(slab_kernel, chips, window),
        out_shape=(
            jax.ShapeDtypeStruct((tokens, heads_width), bf16),
            jax.ShapeDtypeStruct((tokens, width), bf16),
            jax.ShapeDtypeStruct((tokens, width), bf16),
        ),
        in_specs=[pl.BlockSpec(memory_space=pltpu.SMEM)] + [vmem] * 8 + [hbm] * 3,
        out_specs=(vmem, vmem, vmem),
        scratch_shapes=[
            pltpu.VMEM((window + 2, tokens, 2 * kvw), bf16),
            pltpu.VMEM((KEY_VALUE_HEADS, group_rows, HEAD_SIZE), bf16),
            pltpu.VMEM((KEY_VALUE_HEADS, 1, group_rows), f32),
            pltpu.VMEM((KEY_VALUE_HEADS, 1, group_rows), f32),
            pltpu.VMEM((KEY_VALUE_HEADS, HEAD_SIZE, group_rows), f32),
            pltpu.VMEM((QUERY_HEADS, tokens, HEAD_SIZE), bf16),
            pltpu.VMEM((blocks, out_weight.shape[0], width), bf16),
            pltpu.VMEM((tokens, width), f32),
            pltpu.VMEM((chips, 2, tokens), f32),
            pltpu.VMEM((chips, 2, tokens), f32),
            pltpu.VMEM((tokens, 128), f32),
            pltpu.VMEM((width, 4 * ff), bf16),
            pltpu.VMEM((2 * ff, width), bf16),
            pltpu.VMEM((2, chips, half, width), bf16),
            pltpu.VMEM((2, chips + 1, half, width), bf16),
            pltpu.VMEM((tokens, width), f32),
            pltpu.VMEM((tokens, width), f32),
            dma((window // 2,)),
            dma((window // 2,)),
            dma((window // 2,)),
            dma((window // 2,)),
            dma((8,)),
            dma,
            dma((2, chips // 2)),
            dma((2, chips // 2)),
            dma((2, chips // 2 + 1)),
            dma((2, chips // 2 + 1)),
            dma((chips,)),
            dma((chips,)),
            dma((3,)),
            dma((3,)),
            dma((3,)),
            dma((2, chips)),
            dma((2, chips)),
            dma((2, chips)),
            dma((2, chips)),
        ],
        compiler_params=pltpu.CompilerParams(
            collective_id=0, has_side_effects=True, vmem_limit_bytes=48 << 20
        ),
    )(
        doc_of_block,
        queries,
        token_key_heads,
        token_value_heads,
        residual,
        out_weight,
        norm_gain.reshape(1, width),
        expert_ids,
        gate_weights,
        w_gate,
        w_up,
        w_down,
    )


def solution(mesh):
    in_specs = (
        P(("pack", "seq"), None),
        P(("pack", "seq"), None),
        P(("pack", "seq"), None),
        P(("pack", "seq"), None),
        P("seq", None),
        P(),
        P("seq", None, None),
        P("seq", None, None),
        P("seq", None, None),
        P(("pack", "seq"), None),
        P(("pack", "seq"), None),
        P("pack"),
    )
    out_specs = (P(("pack", "seq"), None), P(("pack", "seq"), None), P(("pack", "seq"), None))
    return jax.shard_map(shards, mesh=mesh, in_specs=in_specs, out_specs=out_specs, check_vma=False)
```

```python
import functools
import math

import jax
import jax.numpy as jnp
from jax import lax
from jax.experimental import pallas as pl
from jax.experimental.pallas import tpu as pltpu
from jax.sharding import PartitionSpec as P

QUERY_HEADS = 16
KEY_VALUE_HEADS = 2
HEAD_SIZE = 128
TOP = 8
MESH = pl.DeviceIdType.MESH
HIDE = -1e30


def slab_kernel(
    chips,
    side,
    window,
    doc_ref,
    q_hbm,
    k_hbm,
    v_hbm,
    res_hbm,
    wo_hbm,
    gain_ref,
    ids_hbm,
    gw_hbm,
    wg_hbm,
    wu_hbm,
    wd_hbm,
    attn_out,
    hid_out,
    mix_out,
    kv,
    qs,
    run_max,
    run_sum,
    oacc,
    heads,
    wfull,
    res_in,
    ids_in,
    gw_in,
    hidden,
    gate_send,
    gates,
    gate_cols,
    wgu,
    wd,
    far_gu,
    far_d,
    relay_gu,
    relay_d,
    xown,
    xbuf,
    accbuf,
    home,
    contrib,
    own_part,
    in_s,
    kv_s,
    kv_r,
    sib_s,
    sib_r,
    first_s,
    first_r,
    z_s,
    z_r,
    p_s,
    p_r,
    f_s,
    f_r,
    wsib_s,
    wsib_r,
    g_s,
    g_r,
    load_s,
    ew_s,
    ew_r,
    leg_s,
    leg_r,
    o_s,
    o_r,
    os_s,
    os_r,
    x_s,
    x_r,
    a_s,
    a_r,
    h_s,
    h_r,
):
    me = lax.axis_index("seq")
    chip, core = me // 2, me % 2
    sib = chip * 2 + (1 - core)
    group = QUERY_HEADS // KEY_VALUE_HEADS
    tokens, width = res_hbm.shape
    half = tokens // 2
    kvw = k_hbm.shape[1]
    pack = lax.axis_index("pack")
    col_at, row_at = pack % side, pack // side
    w_rows = wo_hbm.shape[0]
    piece = width // (2 * side)
    mid = chips // 2
    ff = wg_hbm.shape[2]
    hops = window // 2
    first = window + 1
    reach = chips // 4

    def wrap(c):
        return lax.rem(c + 4 * chips, chips)

    def at(c):
        return wrap(c) * 2 + core

    nxt, prv = at(chip + 1), at(chip - 1)

    def rcopy(src, dst, ssem, rsem, dev, whole=False):
        return pltpu.make_async_remote_copy(
            src_ref=src,
            dst_ref=dst,
            send_sem=ssem,
            recv_sem=rsem,
            device_id=dev if whole else {"seq": dev},
            device_id_type=MESH,
        )

    def kv_hop(t, part):
        wide = pl.ds(part * kvw, kvw)
        return rcopy(
            kv.at[2 * t, :, wide],
            kv.at[2 * t + 2, :, wide],
            kv_s.at[t, part],
            kv_r.at[t, part],
            nxt,
        )

    def kv_share(t):
        return rcopy(
            kv.at[2 * t], kv.at[2 * (t - core) + 1], sib_s.at[t - core], sib_r.at[t - core], sib
        )

    def kv_shared(t):
        return rcopy(kv.at[2 * t + 1], kv.at[2 * t + 1], sib_s.at[t], sib_r.at[t], sib)

    def place(d, h):
        return mid - h if d == 0 else mid + h

    def wide_of(half_at, quarter):
        start = (half_at * side + lax.rem(quarter + side, side)) * piece
        return pl.ds(pl.multiple_of(start, 128), piece)

    def own_wide(half_at):
        return wide_of(half_at, col_at if half_at == 0 else row_at)

    def z_hop(d, h, half_at):
        wide = own_wide(half_at)
        return rcopy(
            wfull.at[place(d, h), core, :, wide],
            wfull.at[place(d, h + 1), core, :, wide],
            z_s.at[d, h, half_at],
            z_r.at[d, h, half_at],
            nxt if d == 0 else prv,
        )

    def pair(t, d):
        return pl.ds(mid - 2 * t if d == 0 else mid + 2 * t - 1, 2)

    def beside(q):
        step = 1 - 2 * (q % 2)
        if q < 2:
            return {"pack": row_at * side + lax.rem(col_at + step + side, side)}
        return {"pack": lax.rem(row_at + step + side, side) * side + col_at}

    def wide_from(q, distance):
        step = 1 - 2 * (q % 2)
        mine = col_at if q < 2 else row_at
        return wide_of(q // 2, mine - step * distance)

    def plane_copy(t, d, q):
        ref = wfull.at[pair(t, d), core, :, own_wide(q // 2)]
        return rcopy(ref, ref, p_s.at[t - 1, d, q], p_r.at[t - 1, d, q], beside(q), whole=True)

    def plane_arrived(t, d, q):
        ref = wfull.at[pair(t, d), core, :, wide_from(q, 1)]
        return rcopy(ref, ref, p_s.at[t - 1, d, q], p_r.at[t - 1, d, q], beside(q), whole=True)

    def far_rows(q):
        return pl.ds((q % 2) * (w_rows // 2), w_rows // 2)

    def far_copy(t, d, q):
        ref = wfull.at[pair(t, d), core, far_rows(q), wide_from(q, 1)]
        return rcopy(ref, ref, f_s.at[t - 1, d, q], f_r.at[t - 1, d, q], beside(q), whole=True)

    def far_arrived(t, d, q):
        ref = wfull.at[pair(t, d), core, far_rows(q), wide_from(q, 2)]
        return rcopy(ref, ref, f_s.at[t - 1, d, q], f_r.at[t - 1, d, q], beside(q), whole=True)

    def w_share(t, d):
        ref = wfull.at[pair(t, d), core]
        return rcopy(ref, ref, wsib_s.at[t, d], wsib_r.at[t, d], sib)

    def w_shared(t, d):
        ref = wfull.at[pair(t, d), 1 - core]
        return rcopy(ref, ref, wsib_s.at[t, d], wsib_r.at[t, d], sib)

    def own_share():
        ref = wfull.at[mid, core]
        return rcopy(ref, ref, wsib_s.at[0, 0], wsib_r.at[0, 0], sib)

    def own_shared():
        ref = wfull.at[mid, 1 - core]
        return rcopy(ref, ref, wsib_s.at[0, 0], wsib_r.at[0, 0], sib)

    def gate_copy(r):
        to = wrap(chip + reach - r)
        return rcopy(gate_send.at[to], gates.at[r], g_s.at[r], g_r.at[r], to * 2 + core)

    def first_copy(n, dev):
        return rcopy(kv.at[first], kv.at[first], first_s.at[n], first_r, dev)

    def cols(e):
        return pl.ds(pl.multiple_of(e * ff, 128), ff)

    def up_cols(e):
        return pl.ds(pl.multiple_of((2 + e) * ff, 128), ff)

    def rows(e):
        return pl.ds(pl.multiple_of(e * ff, 128), ff)

    weights = (
        (wg_hbm.at[0], wgu.at[:, cols(core)], wgu.at[:, cols(1 - core)]),
        (wu_hbm.at[0], wgu.at[:, up_cols(core)], wgu.at[:, up_cols(1 - core)]),
        (wd_hbm.at[0], wd.at[rows(core)], wd.at[rows(1 - core)]),
    )

    def piece_of(gu, down, n, major, minor=None, cut=None):
        if n % 2 == 0:
            count = width // side
            start = major * count
            if minor is not None:
                count = count // side
                start = start + minor * count
            if cut is not None:
                count = count // 2
                start = start + cut * count
            return gu.at[
                pl.ds(pl.multiple_of(start, 16), count), cols(core) if n == 0 else up_cols(core)
            ]
        count = ff // (2 * side)
        start = core * ff + (n // 2) * (ff // 2) + major * count
        wide, first_col = width, 0
        if minor is not None:
            wide = width // side
            first_col = minor * wide
        if cut is not None:
            wide = wide // 2
            first_col = first_col + cut * wide
        return down.at[
            pl.ds(pl.multiple_of(start, 16), count), pl.ds(pl.multiple_of(first_col, 128), wide)
        ]

    def minor_at(n):
        return col_at if n < 2 else row_at

    def major_at(n):
        return row_at if n < 2 else col_at

    def turn(at_now, by):
        return lax.rem(at_now + by + side, side)

    def leg(n, second):
        to = at(chip + reach) if n < 2 else at(chip - reach)
        held = relay_gu.at[n // 2] if n % 2 == 0 else relay_d.at[n // 2]
        if second:
            dst = piece_of(far_gu, far_d, n, major_at(n), minor_at(n))
            return rcopy(held, dst, leg_s.at[1, n], leg_r.at[1, n], to)
        src = piece_of(wgu, wd, n, major_at(n), minor_at(n))
        return rcopy(src, held, leg_s.at[0, n], leg_r.at[0, n], to)

    def opposite(stage, n, b, came=False):
        step = 1 - 2 * b
        over_x = (n < 2) == (stage < 2)
        q = b if over_x else 2 + b
        back = (stage % 2 + came) * -step
        cut = b if stage % 2 else None
        if stage < 2:
            ref = piece_of(far_gu, far_d, n, major_at(n), turn(minor_at(n), back), cut)
        else:
            ref = piece_of(far_gu, far_d, n, turn(major_at(n), back), None, cut)
        return rcopy(ref, ref, o_s.at[stage, n, b], o_r.at[stage, n, b], beside(q), whole=True)

    def opposite_step(stage):
        for n in range(4):
            if stage == 0:
                leg(n, True).wait_recv()
            if stage == 2:
                for b in range(2):
                    opposite(1, n, b, True).wait_recv()
            for b in range(2):
                if stage % 2:
                    opposite(stage - 1, n, b, True).wait_recv()
                opposite(stage, n, b).start()

    def opposite_share(mine):
        which = core if mine else 1 - core
        refs = (far_gu.at[:, cols(which)], far_gu.at[:, up_cols(which)], far_d.at[rows(which)])
        return [rcopy(r, r, os_s.at[n], os_r.at[n], sib) for n, r in enumerate(refs)]

    def unit(q, h):
        return 2 * (h - 1) + q if h < reach else 2 * (reach - 1)

    def far_end(d, q):
        return reach if d == q else reach - 1

    def x_hop(d, q, h):
        src = xown.at[q] if h == 0 else xbuf.at[unit(q, h), d]
        to = unit(q, h + 1)
        return rcopy(src, xbuf.at[to, d], x_s.at[to, d], x_r.at[to, d], nxt if d == 0 else prv)

    def a_hop(d, q, h):
        u = unit(q, h)
        to = prv if d == 0 else nxt
        if h == 1:
            return rcopy(accbuf.at[u, d], home.at[d, q], h_s.at[d, q], h_r.at[d, q], to)
        v = unit(q, h - 1)
        return rcopy(accbuf.at[u, d], accbuf.at[v, d], a_s.at[v, d], a_r.at[v, d], to)

    takes = [
        (k_hbm, kv.at[0, :, pl.ds(0, kvw)]),
        (v_hbm, kv.at[0, :, pl.ds(kvw, kvw)]),
        (wo_hbm, wfull.at[mid, core]),
        (ids_hbm, ids_in),
        (gw_hbm, gw_in),
    ]
    for h in range(QUERY_HEADS):
        takes.append(
            (
                q_hbm.at[:, pl.ds(h * HEAD_SIZE, HEAD_SIZE)],
                qs.at[h // group, pl.ds((h % group) * tokens, tokens)],
            )
        )
    takes.append((res_hbm, res_in))
    takes = [
        pltpu.make_async_copy(src, dst, in_s.at[n]) for n, (src, dst) in enumerate(takes)
    ]
    for take in takes:
        take.start()
    for n, (src, mine, _) in enumerate(weights):
        pltpu.make_async_copy(src, mine, load_s.at[n]).start()

    barrier = pltpu.get_barrier_semaphore()

    def greet(d, carry):
        pl.semaphore_signal(
            barrier, inc=1, device_id={"seq": at(chip + d)}, device_id_type=MESH
        )
        return carry

    lax.fori_loop(1, chips, greet, 0)
    pl.semaphore_signal(barrier, inc=1, device_id={"seq": sib}, device_id_type=MESH)
    for q in range(4):
        pl.semaphore_signal(barrier, inc=1, device_id=beside(q), device_id_type=MESH)
    for take in takes[:3]:
        take.wait()
    pl.semaphore_wait(barrier, chips + 4)

    for half_at in range(2):
        z_hop(1, 0, half_at).start()
        z_hop(0, 0, half_at).start()
    for part in range(2):
        kv_hop(0, part).start()

    @pl.when(core == 0)
    def _():
        kv_share(0).start()

    reached = tuple(range(chips - 1, 4, -2))

    @pl.when(me == 0)
    def _():
        for n, c in enumerate(reached):
            rcopy(kv.at[0], kv.at[first], first_s.at[n], first_r, 2 * c).start()

    own_share().start()

    @pl.when(chip < 4)
    def _():
        kv[first] = kv[0]

    for take in takes[3:]:
        take.wait()
    expert = lax.broadcasted_iota(jnp.int32, (2 * chips, tokens), 0)
    by_expert = jnp.zeros((2 * chips, tokens), jnp.float32)
    for n in range(TOP):
        by_expert = by_expert + jnp.where(
            expert == ids_in[n : n + 1, :], gw_in[n : n + 1, :], 0.0
        )
    for c in range(chips):
        far = (c + chips // 2) % chips
        gate_send[c] = jnp.concatenate(
            [by_expert[2 * c : 2 * c + 2], by_expert[2 * far : 2 * far + 2]], axis=0
        )
    gates[reach] = gate_send[chip]
    others = [r for r in range(2 * reach + 1) if r != reach]
    for r in others:
        gate_copy(r).start()

    run_max[...] = jnp.full_like(run_max, HIDE)
    run_sum[...] = jnp.zeros_like(run_sum)
    oacc[...] = jnp.zeros_like(oacc)
    factor = 1.0 / HEAD_SIZE**0.5

    def attend(slot, seen):
        key_at = lax.broadcasted_iota(jnp.int32, (tokens, tokens), 0)
        query_at = lax.broadcasted_iota(jnp.int32, (tokens, tokens), 1)
        bias = jnp.where(seen, 0.0, HIDE).astype(jnp.float32)
        late = (key_at > query_at) & (slot == 0)
        tile = jnp.where(late, HIDE, bias)
        tile = jnp.concatenate([tile] * group, axis=1)
        for g in range(KEY_VALUE_HEADS):
            keys = kv[slot, :, g * HEAD_SIZE : (g + 1) * HEAD_SIZE]
            values = kv[slot, :, kvw + g * HEAD_SIZE : kvw + (g + 1) * HEAD_SIZE]
            s = lax.dot_general(
                keys, qs[g], (((1,), (1,)), ((), ())), preferred_element_type=jnp.float32
            )
            s = s * factor + tile
            old = run_max[g]
            new = jnp.maximum(old, jnp.max(s, axis=0, keepdims=True))
            p = jnp.exp(s - new)
            fade = jnp.exp(old - new)
            run_max[g] = new
            run_sum[g] = run_sum[g] * fade + jnp.sum(p, axis=0, keepdims=True)
            oacc[g] = oacc[g] * fade + lax.dot_general(
                values,
                p.astype(jnp.bfloat16),
                (((0,), (0,)), ((), ())),
                preferred_element_type=jnp.float32,
            )

    own_doc = doc_ref[me]

    def seen_of(slot):
        blk = me - slot
        doc = doc_ref[jnp.maximum(blk, 0)]
        return (blk == 0) | ((blk > 0) & (doc == own_doc))

    def z_step(h):
        for d in range(2):
            for half_at in range(2):
                z_hop(d, h - 1, half_at).wait_recv()

                @pl.when(h < mid)
                def _():
                    z_hop(d, h, half_at).start()

    def each(action):
        for d in range(2):
            for q in range(4):
                action(d, q)

    def plane_step(t):
        each(lambda d, q: plane_copy(t, d, q).start())

    def far_step(t):
        def one(d, q):
            plane_arrived(t, d, q).wait_recv()
            far_copy(t, d, q).start()

        each(one)

    def share_step(t):
        each(lambda d, q: far_arrived(t, d, q).wait_recv())
        for d in range(2):
            w_share(t, d).start()

    for n, (src, mine, _) in enumerate(weights):
        pltpu.make_async_copy(src, mine, load_s.at[n]).wait()
        rcopy(mine, mine, ew_s.at[n], ew_r.at[n], sib).start()
    for n in range(4):
        leg(n, False).start()

    attend(0, me >= 0)

    def window_step(t, carry):
        z_step(2 * t - 1)
        for part in range(2):
            kv_hop(t - 1, part).wait_recv()

            @pl.when((t < hops - 1) | (core == 1))
            def _():
                kv_hop(t, part).start()

        kv_share(t).start()

        @pl.when(t > 1)
        def _():
            far_step(t - 1)

        z_step(2 * t)
        plane_step(t)

        @pl.when(t > 2)
        def _():
            share_step(t - 2)

        def both(n, inner):
            slot = 2 * t - n

            @pl.when(n == 1)
            def _():
                kv_shared(t - 1).wait_recv()

            attend(slot, seen_of(slot))
            return inner

        lax.fori_loop(0, 2, both, 0)

        @pl.when(t == 2)
        def _():
            for n in range(4):
                leg(n, False).wait_recv()
                leg(n, True).start()

        @pl.when((t == 2) & (core == 0) & (chip >= 5) & (chip % 2 == 1))
        def _():
            first_copy(0, sib).wait_recv()
            first_copy(0, at(chip - 1)).start()
            first_copy(1, sib).start()

        @pl.when((t == 3) & (core == 0) & (chip >= 4) & (chip % 2 == 0))
        def _():
            first_copy(1, sib).wait_recv()
            first_copy(1, sib).start()

        return carry

    lax.fori_loop(1, hops, window_step, 0)

    z_step(2 * hops - 1)

    @pl.when(core == 1)
    def _():
        for part in range(2):
            kv_hop(hops - 1, part).wait_recv()
        kv_share(hops).start()

    far_step(hops - 1)
    z_step(2 * hops)
    plane_step(hops)
    share_step(hops - 2)
    opposite_step(0)
    kv_shared(hops - 1).wait_recv()

    @pl.when((core == 1) & (chip >= 4))
    def _():
        first_copy(0, sib).wait_recv()

    def rest(n, carry):
        slot = window - 1 + 2 * n
        attend(slot, ((n == 0) & seen_of(window - 1)) | ((n == 1) & (me >= window)))
        return carry

    lax.fori_loop(0, 2, rest, 0)

    far_step(hops)
    share_step(hops - 1)
    opposite_step(1)

    for g in range(KEY_VALUE_HEADS):
        done = oacc[g] / run_sum[g]
        for n in range(group):
            h = g * group + n
            one = done[:, n * tokens : (n + 1) * tokens].T.astype(jnp.bfloat16)
            attn_out[:, h * HEAD_SIZE : (h + 1) * HEAD_SIZE] = one
            heads[h] = one

    own_shared().wait_recv()
    hidden[...] = res_in[...].astype(jnp.float32) + jnp.dot(
        heads[chip],
        wfull[mid].reshape(2 * w_rows, width),
        preferred_element_type=jnp.float32,
    )

    opposite_step(2)

    def project(t, d):
        at_pair = mid - 2 * t if d == 0 else mid + 2 * t - 1
        one = wrap(chip + at_pair - mid)
        left = heads[one]
        if d == 0:
            left = jnp.where(t == hops, jnp.zeros_like(left), left)
        both = jnp.concatenate([left, heads[wrap(one + 1)]], axis=1)
        hidden[...] += jnp.dot(
            both,
            wfull[pl.ds(at_pair, 2)].reshape(4 * w_rows, width),
            preferred_element_type=jnp.float32,
        )

    def project_step(t, carry):
        for d in range(2):
            w_shared(t, d).wait_recv()
            project(t, d)

        @pl.when(t == 1)
        def _():
            share_step(hops)

        return carry

    lax.fori_loop(1, hops + 1, project_step, 0)

    state = hidden[...]
    hid_out[...] = state.astype(jnp.bfloat16)
    mean_square = jnp.mean(state * state, axis=-1, keepdims=True)
    normed = (
        state * lax.rsqrt(mean_square + 1e-06) * gain_ref[...].astype(jnp.float32).reshape(1, width)
    ).astype(jnp.bfloat16)
    for q in range(2):
        xown[q] = normed[q * half : (q + 1) * half]
    for q in range(2):
        for d in range(2):
            x_hop(d, q, 0).start()
    opposite_step(3)

    for r in others:
        gate_copy(r).wait_recv()
    lane = lax.broadcasted_iota(jnp.int32, (half, 128), 1)
    stacked = jnp.concatenate(
        [gates[r] for r in range(2 * reach + 1)]
        + [jnp.zeros((128 - 4 * (2 * reach + 1), tokens), jnp.float32)],
        axis=0,
    )
    gate_cols[...] = stacked.T
    for n, (_, _, theirs) in enumerate(weights):
        rcopy(theirs, theirs, ew_s.at[n], ew_r.at[n], sib).wait_recv()

    def served(x, places, halves, far):
        gu, down = (far_gu, far_d) if far else (wgu, wd)
        both = jnp.dot(x, gu[...], preferred_element_type=jnp.float32)
        parts = []
        for e in range(2):
            gate = []
            for d in range(2):
                at_rows = pl.ds(pl.multiple_of(halves[d] * half, half), half)
                column = 4 * places[d] + 2 * far + e
                gate.append(
                    jnp.sum(
                        jnp.where(lane == column, gate_cols[at_rows, :], 0.0),
                        axis=1,
                        keepdims=True,
                    )
                )
            gate = jnp.concatenate(gate, axis=0)
            v = both[:, e * ff : (e + 1) * ff]
            u = both[:, (2 + e) * ff : (3 + e) * ff]
            parts.append((v / (1.0 + jnp.exp(-v)) * u * gate).astype(jnp.bfloat16))
        return jnp.dot(
            jnp.concatenate(parts, axis=1), down[...], preferred_element_type=jnp.float32
        )

    def own_served(far):
        return served(xown[...].reshape(tokens, width), (reach, reach), (0, 1), far)

    def unit_served(u, far):
        h = u // 2 + 1
        last = u == 2 * (reach - 1)
        halves = [jnp.where(last, d, u % 2) for d in range(2)]
        return served(xbuf[u].reshape(tokens, width), (reach - h, reach + h), halves, far)

    def take_x(h):
        for q in range(2):
            for d in range(2):
                if h <= far_end(d, q):
                    x_hop(d, q, h - 1).wait_recv()
                if h < far_end(d, q):
                    x_hop(d, q, h).start()

    def natural(u, carry):
        contrib[u] = unit_served(u, 0)
        return carry

    def opposed(u, carry):
        contrib[u] += unit_served(u, 1)
        return carry

    def send_sum(d, q, h):
        u = unit(q, h)
        part = contrib[u, d * half : (d + 1) * half]
        if h < far_end(d, q):
            a_hop(d, q, h + 1).wait_recv()
            part = part + accbuf[u, d].astype(jnp.float32)
        accbuf[u, d] = part.astype(jnp.bfloat16)
        a_hop(d, q, h).start()

    own_part[...] = own_served(0)
    take_x(1)
    lax.fori_loop(0, 2, natural, 0)
    for n in range(4):
        for b in range(2):
            opposite(3, n, b, True).wait_recv()
    for copy in opposite_share(True):
        copy.start()
    take_x(2)
    lax.fori_loop(2, 4, natural, 0)
    for copy in opposite_share(False):
        copy.wait_recv()
    take_x(3)
    lax.fori_loop(4, 6, natural, 0)
    lax.fori_loop(4, 6, opposed, 0)
    send_sum(0, 1, 3)
    send_sum(1, 0, 3)
    take_x(4)
    lax.fori_loop(6, 7, natural, 0)
    lax.fori_loop(6, 7, opposed, 0)
    send_sum(0, 0, 4)
    send_sum(1, 1, 4)
    lax.fori_loop(2, 4, opposed, 0)
    send_sum(0, 1, 2)
    send_sum(1, 0, 2)
    send_sum(0, 0, 3)
    send_sum(1, 1, 3)
    lax.fori_loop(0, 2, opposed, 0)
    send_sum(0, 1, 1)
    send_sum(1, 0, 1)
    send_sum(0, 0, 2)
    send_sum(1, 1, 2)
    own_part[...] += own_served(1)
    send_sum(0, 0, 1)
    send_sum(1, 1, 1)
    for q in range(2):
        part = slice(q * half, (q + 1) * half)
        total = own_part[part]
        for d in (1 - q, q):
            a_hop(d, q, 1).wait_recv()
            total = total + home[d, q].astype(jnp.float32)
        mix_out[part] = total.astype(jnp.bfloat16)

    for part in range(2):
        for t in range(hops - 1):
            kv_hop(t, part).wait_send()

        @pl.when(core == 1)
        def _():
            kv_hop(hops - 1, part).wait_send()

    for t in range(hops):
        kv_shared(t).wait_send()

    @pl.when(me == 0)
    def _():
        for n in range(len(reached)):
            first_copy(n, sib).wait_send()

    @pl.when((core == 0) & (chip >= 4))
    def _():
        first_copy(1, sib).wait_send()

    @pl.when((core == 0) & (chip >= 5) & (chip % 2 == 1))
    def _():
        first_copy(0, sib).wait_send()

    def sent_z(h, carry):
        for d in range(2):
            for half_at in range(2):
                z_hop(d, h, half_at).wait_send()
        return carry

    lax.fori_loop(0, mid, sent_z, 0)

    def sent_plane(t, carry):
        each(lambda d, q: plane_copy(t, d, q).wait_send())
        each(lambda d, q: far_copy(t, d, q).wait_send())
        for d in range(2):
            w_share(t, d).wait_send()
        return carry

    lax.fori_loop(1, hops + 1, sent_plane, 0)
    own_share().wait_send()

    for r in others:
        gate_copy(r).wait_send()
    for n in range(4):
        for second in (False, True):
            leg(n, second).wait_send()
        for stage in range(4):
            for b in range(2):
                opposite(stage, n, b).wait_send()
    for copy in opposite_share(True):
        copy.wait_send()
    for q in range(2):
        for d in range(2):
            for h in range(far_end(d, q)):
                x_hop(d, q, h).wait_send()
                a_hop(d, q, h + 1).wait_send()
    for n, (_, mine, _) in enumerate(weights):
        rcopy(mine, mine, ew_s.at[n], ew_r.at[n], sib).wait_send()


def shards(
    queries,
    token_key_heads,
    token_value_heads,
    residual,
    out_weight,
    norm_gain,
    w_gate,
    w_up,
    w_down,
    expert_ids,
    gate_weights,
    doc_of_block,
):
    blocks = lax.axis_size("seq")
    chips = blocks // 2
    tokens, width = residual.shape
    heads_width = queries.shape[1]
    kvw = token_key_heads.shape[1]
    ff = w_gate.shape[2]
    window = 8
    side = math.isqrt(lax.axis_size("pack"))
    hops = window // 2
    reach = chips // 4
    units = 2 * reach - 1
    group_rows = tokens * QUERY_HEADS // KEY_VALUE_HEADS
    half = tokens // 2
    vmem = pl.BlockSpec(memory_space=pltpu.VMEM)
    hbm = pl.BlockSpec(memory_space=pltpu.HBM)
    dma = pltpu.SemaphoreType.DMA
    bf16, f32 = jnp.bfloat16, jnp.float32
    return pl.pallas_call(
        functools.partial(slab_kernel, chips, side, window),
        out_shape=(
            jax.ShapeDtypeStruct((tokens, heads_width), bf16),
            jax.ShapeDtypeStruct((tokens, width), bf16),
            jax.ShapeDtypeStruct((tokens, width), bf16),
        ),
        in_specs=[pl.BlockSpec(memory_space=pltpu.SMEM)] + [hbm] * 5 + [vmem] + [hbm] * 5,
        out_specs=(vmem, vmem, vmem),
        scratch_shapes=[
            pltpu.VMEM((window + 2, tokens, 2 * kvw), bf16),
            pltpu.VMEM((KEY_VALUE_HEADS, group_rows, HEAD_SIZE), bf16),
            pltpu.VMEM((KEY_VALUE_HEADS, 1, group_rows), f32),
            pltpu.VMEM((KEY_VALUE_HEADS, 1, group_rows), f32),
            pltpu.VMEM((KEY_VALUE_HEADS, HEAD_SIZE, group_rows), f32),
            pltpu.VMEM((QUERY_HEADS, tokens, HEAD_SIZE), bf16),
            pltpu.VMEM((chips + 1, 2, out_weight.shape[0], width), bf16),
            pltpu.VMEM((tokens, width), bf16),
            pltpu.VMEM((TOP, tokens), jnp.int32),
            pltpu.VMEM((TOP, tokens), f32),
            pltpu.VMEM((tokens, width), f32),
            pltpu.VMEM((chips, 4, tokens), f32),
            pltpu.VMEM((2 * reach + 1, 4, tokens), f32),
            pltpu.VMEM((tokens, 128), f32),
            pltpu.VMEM((width, 4 * ff), bf16),
            pltpu.VMEM((2 * ff, width), bf16),
            pltpu.VMEM((width, 4 * ff), bf16),
            pltpu.VMEM((2 * ff, width), bf16),
            pltpu.VMEM((2, width // side**2, ff), bf16),
            pltpu.VMEM((2, ff // (2 * side), width // side), bf16),
            pltpu.VMEM((2, half, width), bf16),
            pltpu.VMEM((units, 2, half, width), bf16),
            pltpu.VMEM((units, 2, half, width), bf16),
            pltpu.VMEM((2, 2, half, width), bf16),
            pltpu.VMEM((units, tokens, width), f32),
            pltpu.VMEM((tokens, width), f32),
            dma((6 + QUERY_HEADS,)),
            dma((hops, 2)),
            dma((hops, 2)),
            dma((hops,)),
            dma((hops,)),
            dma((8,)),
            dma,
            dma((2, chips // 2, 2)),
            dma((2, chips // 2, 2)),
            dma((hops, 2, 4)),
            dma((hops, 2, 4)),
            dma((hops, 2, 4)),
            dma((hops, 2, 4)),
            dma((hops + 1, 2)),
            dma((hops + 1, 2)),
            dma((2 * reach + 1,)),
            dma((2 * reach + 1,)),
            dma((3,)),
            dma((3,)),
            dma((3,)),
            dma((2, 4)),
            dma((2, 4)),
            dma((4, 4, 2)),
            dma((4, 4, 2)),
            dma((3,)),
            dma((3,)),
            dma((units, 2)),
            dma((units, 2)),
            dma((units, 2)),
            dma((units, 2)),
            dma((2, 2)),
            dma((2, 2)),
        ],
        compiler_params=pltpu.CompilerParams(
            collective_id=0, has_side_effects=True, vmem_limit_bytes=48 << 20
        ),
    )(
        doc_of_block,
        *(pltpu.with_memory_space_constraint(a, pltpu.HBM) for a in (queries, token_key_heads, token_value_heads, residual, out_weight)),
        norm_gain,
        *(pltpu.with_memory_space_constraint(a, pltpu.HBM) for a in (expert_ids.T, gate_weights.T, w_gate, w_up, w_down)),
    )


def solution(mesh):
    in_specs = (
        P(("pack", "seq"), None),
        P(("pack", "seq"), None),
        P(("pack", "seq"), None),
        P(("pack", "seq"), None),
        P("seq", None),
        P(),
        P("seq", None, None),
        P("seq", None, None),
        P("seq", None, None),
        P(("pack", "seq"), None),
        P(("pack", "seq"), None),
        P("pack"),
    )
    out_specs = (P(("pack", "seq"), None), P(("pack", "seq"), None), P(("pack", "seq"), None))
    return jax.shard_map(shards, mesh=mesh, in_specs=in_specs, out_specs=out_specs, check_vma=False)
```

```python
import functools
import math

import jax
import jax.numpy as jnp
from jax import lax
from jax.experimental import pallas as pl
from jax.experimental.pallas import tpu as pltpu
from jax.sharding import PartitionSpec as P

QUERY_HEADS = 16
KEY_VALUE_HEADS = 2
HEAD_SIZE = 128
TOP = 8
MESH = pl.DeviceIdType.MESH
HIDE = -1e30


def slab_kernel(
    chips,
    side,
    window,
    doc_ref,
    q_hbm,
    k_hbm,
    v_hbm,
    res_hbm,
    wo_hbm,
    gain_ref,
    ids_hbm,
    gw_hbm,
    wg_hbm,
    wu_hbm,
    wd_hbm,
    attn_out,
    hid_out,
    mix_out,
    kv,
    qs,
    run_max,
    run_sum,
    oacc,
    heads,
    wfull,
    res_in,
    ids_in,
    gw_in,
    hidden,
    gate_send,
    gates,
    gate_cols,
    wgu,
    wd,
    far_gu,
    far_d,
    relay_gu,
    relay_d,
    xown,
    xbuf,
    accbuf,
    home,
    contrib,
    own_part,
    in_s,
    kv_s,
    kv_r,
    sib_s,
    sib_r,
    first_s,
    first_r,
    z_s,
    z_r,
    p_s,
    p_r,
    f_s,
    f_r,
    wsib_s,
    wsib_r,
    g_s,
    g_r,
    load_s,
    ew_s,
    ew_r,
    leg_s,
    leg_r,
    o_s,
    o_r,
    os_s,
    os_r,
    x_s,
    x_r,
    a_s,
    a_r,
    h_s,
    h_r,
):
    me = lax.axis_index("seq")
    chip, core = me // 2, me % 2
    sib = chip * 2 + (1 - core)
    group = QUERY_HEADS // KEY_VALUE_HEADS
    tokens, width = res_hbm.shape
    half = tokens // 2
    kvw = k_hbm.shape[1]
    pack = lax.axis_index("pack")
    col_at, row_at = pack % side, pack // side
    w_rows = wo_hbm.shape[0]
    piece = width // (2 * side)
    mid = chips // 2
    ff = wg_hbm.shape[2]
    hops = window // 2
    first = window + 1
    reach = chips // 4

    def wrap(c):
        return lax.rem(c + 4 * chips, chips)

    def at(c):
        return wrap(c) * 2 + core

    nxt, prv = at(chip + 1), at(chip - 1)

    def rcopy(src, dst, ssem, rsem, dev, whole=False):
        return pltpu.make_async_remote_copy(
            src_ref=src,
            dst_ref=dst,
            send_sem=ssem,
            recv_sem=rsem,
            device_id=dev if whole else {"seq": dev},
            device_id_type=MESH,
        )

    def kv_hop(t, part):
        wide = pl.ds(part * kvw, kvw)
        return rcopy(
            kv.at[2 * t, :, wide],
            kv.at[2 * t + 2, :, wide],
            kv_s.at[t, part],
            kv_r.at[t, part],
            nxt,
        )

    def kv_share(t):
        return rcopy(
            kv.at[2 * t], kv.at[2 * (t - core) + 1], sib_s.at[t - core], sib_r.at[t - core], sib
        )

    def kv_shared(t):
        return rcopy(kv.at[2 * t + 1], kv.at[2 * t + 1], sib_s.at[t], sib_r.at[t], sib)

    def place(d, h):
        return mid - h if d == 0 else mid + h

    def wide_of(half_at, quarter):
        start = (half_at * side + lax.rem(quarter + side, side)) * piece
        return pl.ds(pl.multiple_of(start, 128), piece)

    def own_wide(half_at):
        return wide_of(half_at, col_at if half_at == 0 else row_at)

    def z_hop(d, h, half_at):
        wide = own_wide(half_at)
        return rcopy(
            wfull.at[place(d, h), core, :, wide],
            wfull.at[place(d, h + 1), core, :, wide],
            z_s.at[d, h, half_at],
            z_r.at[d, h, half_at],
            nxt if d == 0 else prv,
        )

    def pair(t, d):
        return pl.ds(mid - 2 * t if d == 0 else mid + 2 * t - 1, 2)

    def beside(q):
        step = 1 - 2 * (q % 2)
        if q < 2:
            return {"pack": row_at * side + lax.rem(col_at + step + side, side)}
        return {"pack": lax.rem(row_at + step + side, side) * side + col_at}

    def wide_from(q, distance):
        step = 1 - 2 * (q % 2)
        mine = col_at if q < 2 else row_at
        return wide_of(q // 2, mine - step * distance)

    def plane_copy(t, d, q):
        ref = wfull.at[pair(t, d), core, :, own_wide(q // 2)]
        return rcopy(ref, ref, p_s.at[t - 1, d, q], p_r.at[t - 1, d, q], beside(q), whole=True)

    def plane_arrived(t, d, q):
        ref = wfull.at[pair(t, d), core, :, wide_from(q, 1)]
        return rcopy(ref, ref, p_s.at[t - 1, d, q], p_r.at[t - 1, d, q], beside(q), whole=True)

    def far_rows(q):
        return pl.ds((q % 2) * (w_rows // 2), w_rows // 2)

    def far_copy(t, d, q):
        ref = wfull.at[pair(t, d), core, far_rows(q), wide_from(q, 1)]
        return rcopy(ref, ref, f_s.at[t - 1, d, q], f_r.at[t - 1, d, q], beside(q), whole=True)

    def far_arrived(t, d, q):
        ref = wfull.at[pair(t, d), core, far_rows(q), wide_from(q, 2)]
        return rcopy(ref, ref, f_s.at[t - 1, d, q], f_r.at[t - 1, d, q], beside(q), whole=True)

    def two_over(half_at):
        if half_at == 0:
            return {"pack": row_at * side + lax.rem(col_at + 2, side)}
        return {"pack": lax.rem(row_at + 2, side) * side + col_at}

    def skip_copy(d, half_at, came=False):
        wide = wide_from(2 * half_at, 2) if came else own_wide(half_at)
        ref = wfull.at[pair(hops, d), core, :, wide]
        sems = f_s.at[hops - 1, d, 2 * half_at], f_r.at[hops - 1, d, 2 * half_at]
        return rcopy(ref, ref, *sems, two_over(half_at), whole=True)

    def w_share(t, d):
        ref = wfull.at[pair(t, d), core]
        return rcopy(ref, ref, wsib_s.at[t, d], wsib_r.at[t, d], sib)

    def w_shared(t, d):
        ref = wfull.at[pair(t, d), 1 - core]
        return rcopy(ref, ref, wsib_s.at[t, d], wsib_r.at[t, d], sib)

    def own_share():
        ref = wfull.at[mid, core]
        return rcopy(ref, ref, wsib_s.at[0, 0], wsib_r.at[0, 0], sib)

    def own_shared():
        ref = wfull.at[mid, 1 - core]
        return rcopy(ref, ref, wsib_s.at[0, 0], wsib_r.at[0, 0], sib)

    def gate_copy(r):
        to = wrap(chip + reach - r)
        return rcopy(gate_send.at[to], gates.at[r], g_s.at[r], g_r.at[r], to * 2 + core)

    def first_copy(n, dev):
        return rcopy(kv.at[first], kv.at[first], first_s.at[n], first_r, dev)

    def cols(e):
        return pl.ds(pl.multiple_of(e * ff, 128), ff)

    def up_cols(e):
        return pl.ds(pl.multiple_of((2 + e) * ff, 128), ff)

    def rows(e):
        return pl.ds(pl.multiple_of(e * ff, 128), ff)

    weights = (
        (wg_hbm.at[0], wgu.at[:, cols(core)], wgu.at[:, cols(1 - core)]),
        (wu_hbm.at[0], wgu.at[:, up_cols(core)], wgu.at[:, up_cols(1 - core)]),
        (wd_hbm.at[0], wd.at[rows(core)], wd.at[rows(1 - core)]),
    )

    def piece_of(gu, down, n, major, minor=None, cut=None):
        if n % 2 == 0:
            count = width // side
            start = major * count
            if minor is not None:
                count = count // side
                start = start + minor * count
            if cut is not None:
                count = count // 2
                start = start + cut * count
            return gu.at[
                pl.ds(pl.multiple_of(start, 16), count), cols(core) if n == 0 else up_cols(core)
            ]
        count = ff // (2 * side)
        start = core * ff + (n // 2) * (ff // 2) + major * count
        wide, first_col = width, 0
        if minor is not None:
            wide = width // side
            first_col = minor * wide
        if cut is not None:
            wide = wide // 2
            first_col = first_col + cut * wide
        return down.at[
            pl.ds(pl.multiple_of(start, 16), count), pl.ds(pl.multiple_of(first_col, 128), wide)
        ]

    def minor_at(n):
        return col_at if n < 2 else row_at

    def major_at(n):
        return row_at if n < 2 else col_at

    def turn(at_now, by):
        return lax.rem(at_now + by + side, side)

    def leg(n, second):
        to = at(chip + reach) if n % 2 else at(chip - reach)
        held = relay_gu.at[n // 2] if n % 2 == 0 else relay_d.at[n // 2]
        if second:
            dst = piece_of(far_gu, far_d, n, major_at(n), minor_at(n))
            return rcopy(held, dst, leg_s.at[1, n], leg_r.at[1, n], to)
        src = piece_of(wgu, wd, n, major_at(n), minor_at(n))
        return rcopy(src, held, leg_s.at[0, n], leg_r.at[0, n], to)

    def opposite(stage, n, b, came=False):
        step = 1 - 2 * b
        over_x = (n < 2) == (stage < 2)
        q = b if over_x else 2 + b
        back = (stage % 2 + came) * -step
        cut = b if stage % 2 else None
        if stage < 2:
            ref = piece_of(far_gu, far_d, n, major_at(n), turn(minor_at(n), back), cut)
        else:
            ref = piece_of(far_gu, far_d, n, turn(major_at(n), back), None, cut)
        return rcopy(ref, ref, o_s.at[stage, n, b], o_r.at[stage, n, b], beside(q), whole=True)

    def opposite_step(stage):
        for n in range(4):
            if stage == 0:
                leg(n, True).wait_recv()
            if stage == 2:
                for b in range(2):
                    opposite(1, n, b, True).wait_recv()
            for b in range(2):
                if stage % 2:
                    opposite(stage - 1, n, b, True).wait_recv()
                opposite(stage, n, b).start()

    def opposite_share(mine):
        which = core if mine else 1 - core
        refs = (far_gu.at[:, cols(which)], far_gu.at[:, up_cols(which)], far_d.at[rows(which)])
        return [rcopy(r, r, os_s.at[n], os_r.at[n], sib) for n, r in enumerate(refs)]

    def unit(q, h):
        return 2 * (h - 1) + q if h < reach else 2 * (reach - 1)

    def far_end(d, q):
        return reach if d == q else reach - 1

    def x_hop(d, q, h):
        src = xown.at[q] if h == 0 else xbuf.at[unit(q, h), d]
        to = unit(q, h + 1)
        return rcopy(src, xbuf.at[to, d], x_s.at[to, d], x_r.at[to, d], nxt if d == 0 else prv)

    def a_hop(d, q, h):
        u = unit(q, h)
        to = prv if d == 0 else nxt
        if h == 1:
            return rcopy(accbuf.at[u, d], home.at[d, q], h_s.at[d, q], h_r.at[d, q], to)
        v = unit(q, h - 1)
        return rcopy(accbuf.at[u, d], accbuf.at[v, d], a_s.at[v, d], a_r.at[v, d], to)

    takes = [
        (k_hbm, kv.at[0, :, pl.ds(0, kvw)]),
        (v_hbm, kv.at[0, :, pl.ds(kvw, kvw)]),
        (wo_hbm, wfull.at[mid, core]),
        (ids_hbm, ids_in),
        (gw_hbm, gw_in),
    ]
    for h in range(QUERY_HEADS):
        takes.append(
            (
                q_hbm.at[:, pl.ds(h * HEAD_SIZE, HEAD_SIZE)],
                qs.at[h // group, pl.ds((h % group) * tokens, tokens)],
            )
        )
    takes.append((res_hbm, res_in))
    takes = [
        pltpu.make_async_copy(src, dst, in_s.at[n]) for n, (src, dst) in enumerate(takes)
    ]
    for take in takes:
        take.start()
    for n, (src, mine, _) in enumerate(weights):
        pltpu.make_async_copy(src, mine, load_s.at[n]).start()

    barrier = pltpu.get_barrier_semaphore()

    def greet(d, carry):
        pl.semaphore_signal(
            barrier, inc=1, device_id={"seq": at(chip + d)}, device_id_type=MESH
        )
        return carry

    lax.fori_loop(1, chips, greet, 0)
    pl.semaphore_signal(barrier, inc=1, device_id={"seq": sib}, device_id_type=MESH)
    for q in range(4):
        pl.semaphore_signal(barrier, inc=1, device_id=beside(q), device_id_type=MESH)
    for half_at in range(2):
        pl.semaphore_signal(barrier, inc=1, device_id=two_over(half_at), device_id_type=MESH)
    for take in takes[:3]:
        take.wait()
    pl.semaphore_wait(barrier, chips + 6)

    for half_at in range(2):
        z_hop(1, 0, half_at).start()
        z_hop(0, 0, half_at).start()
    for part in range(2):
        kv_hop(0, part).start()

    @pl.when(core == 0)
    def _():
        kv_share(0).start()

    reached = tuple(range(chips - 1, 4, -2))

    @pl.when(me == 0)
    def _():
        for n, c in enumerate(reached):
            rcopy(kv.at[0], kv.at[first], first_s.at[n], first_r, 2 * c).start()

    own_share().start()

    @pl.when(chip < 4)
    def _():
        kv[first] = kv[0]

    for take in takes[3:]:
        take.wait()
    expert = lax.broadcasted_iota(jnp.int32, (2 * chips, tokens), 0)
    by_expert = jnp.zeros((2 * chips, tokens), jnp.float32)
    for n in range(TOP):
        by_expert = by_expert + jnp.where(
            expert == ids_in[n : n + 1, :], gw_in[n : n + 1, :], 0.0
        )
    for c in range(chips):
        far = (c + chips // 2) % chips
        gate_send[c] = jnp.concatenate(
            [by_expert[2 * c : 2 * c + 2], by_expert[2 * far : 2 * far + 2]], axis=0
        )
    gates[reach] = gate_send[chip]
    others = [r for r in range(2 * reach + 1) if r != reach]
    for r in others:
        gate_copy(r).start()

    run_max[...] = jnp.full_like(run_max, HIDE)
    run_sum[...] = jnp.zeros_like(run_sum)
    oacc[...] = jnp.zeros_like(oacc)
    factor = 1.0 / HEAD_SIZE**0.5

    def attend(slot, seen):
        key_at = lax.broadcasted_iota(jnp.int32, (tokens, tokens), 0)
        query_at = lax.broadcasted_iota(jnp.int32, (tokens, tokens), 1)
        bias = jnp.where(seen, 0.0, HIDE).astype(jnp.float32)
        late = (key_at > query_at) & (slot == 0)
        tile = jnp.where(late, HIDE, bias)
        tile = jnp.concatenate([tile] * group, axis=1)
        for g in range(KEY_VALUE_HEADS):
            keys = kv[slot, :, g * HEAD_SIZE : (g + 1) * HEAD_SIZE]
            values = kv[slot, :, kvw + g * HEAD_SIZE : kvw + (g + 1) * HEAD_SIZE]
            s = lax.dot_general(
                keys, qs[g], (((1,), (1,)), ((), ())), preferred_element_type=jnp.float32
            )
            s = s * factor + tile
            old = run_max[g]
            new = jnp.maximum(old, jnp.max(s, axis=0, keepdims=True))
            p = jnp.exp(s - new)
            fade = jnp.exp(old - new)
            run_max[g] = new
            run_sum[g] = run_sum[g] * fade + jnp.sum(p, axis=0, keepdims=True)
            oacc[g] = oacc[g] * fade + lax.dot_general(
                values,
                p.astype(jnp.bfloat16),
                (((0,), (0,)), ((), ())),
                preferred_element_type=jnp.float32,
            )

    own_doc = doc_ref[me]

    def seen_of(slot):
        blk = me - slot
        doc = doc_ref[jnp.maximum(blk, 0)]
        return (blk == 0) | ((blk > 0) & (doc == own_doc))

    def z_step(h):
        for d in range(2):
            for half_at in range(2):
                z_hop(d, h - 1, half_at).wait_recv()

                @pl.when(h < mid)
                def _():
                    z_hop(d, h, half_at).start()

    def each(action):
        for d in range(2):
            for q in range(4):
                action(d, q)

    def plane_step(t):
        each(lambda d, q: plane_copy(t, d, q).start())

    def far_step(t):
        def one(d, q):
            plane_arrived(t, d, q).wait_recv()
            far_copy(t, d, q).start()

        each(one)

    def share_step(t):
        each(lambda d, q: far_arrived(t, d, q).wait_recv())
        for d in range(2):
            w_share(t, d).start()

    for n, (src, mine, _) in enumerate(weights):
        pltpu.make_async_copy(src, mine, load_s.at[n]).wait()
        rcopy(mine, mine, ew_s.at[n], ew_r.at[n], sib).start()
    for n in range(4):
        leg(n, False).start()

    attend(0, me >= 0)

    def window_step(t, carry):
        z_step(2 * t - 1)
        for part in range(2):
            kv_hop(t - 1, part).wait_recv()

            @pl.when((t < hops - 1) | (core == 1))
            def _():
                kv_hop(t, part).start()

        kv_share(t).start()

        @pl.when(t > 1)
        def _():
            far_step(t - 1)

        z_step(2 * t)
        plane_step(t)

        @pl.when(t > 2)
        def _():
            share_step(t - 2)

        def both(n, inner):
            slot = 2 * t - n

            @pl.when(n == 1)
            def _():
                kv_shared(t - 1).wait_recv()

            attend(slot, seen_of(slot))
            return inner

        lax.fori_loop(0, 2, both, 0)

        @pl.when(t == 2)
        def _():
            for n in range(4):
                leg(n, False).wait_recv()
                leg(n, True).start()

        @pl.when((t == 2) & (core == 0) & (chip >= 5) & (chip % 2 == 1))
        def _():
            first_copy(0, sib).wait_recv()
            first_copy(0, at(chip - 1)).start()
            first_copy(1, sib).start()

        @pl.when((t == 3) & (core == 0) & (chip >= 4) & (chip % 2 == 0))
        def _():
            first_copy(1, sib).wait_recv()
            first_copy(1, sib).start()

        return carry

    lax.fori_loop(1, hops, window_step, 0)

    z_step(2 * hops - 1)

    @pl.when(core == 1)
    def _():
        for part in range(2):
            kv_hop(hops - 1, part).wait_recv()
        kv_share(hops).start()

    far_step(hops - 1)
    z_step(2 * hops)
    plane_step(hops)
    for d in range(2):
        for half_at in range(2):
            skip_copy(d, half_at).start()
    share_step(hops - 2)
    opposite_step(0)
    kv_shared(hops - 1).wait_recv()

    @pl.when((core == 1) & (chip >= 4))
    def _():
        first_copy(0, sib).wait_recv()

    def rest(n, carry):
        slot = window - 1 + 2 * n
        attend(slot, ((n == 0) & seen_of(window - 1)) | ((n == 1) & (me >= window)))
        return carry

    lax.fori_loop(0, 2, rest, 0)

    share_step(hops - 1)
    each(lambda d, q: plane_arrived(hops, d, q).wait_recv())
    for d in range(2):
        for half_at in range(2):
            skip_copy(d, half_at, True).wait_recv()
        w_share(hops, d).start()

    for g in range(KEY_VALUE_HEADS):
        done = oacc[g] / run_sum[g]
        for n in range(group):
            h = g * group + n
            one = done[:, n * tokens : (n + 1) * tokens].T.astype(jnp.bfloat16)
            attn_out[:, h * HEAD_SIZE : (h + 1) * HEAD_SIZE] = one
            heads[h] = one

    own_shared().wait_recv()
    hidden[...] = res_in[...].astype(jnp.float32) + jnp.dot(
        heads[chip],
        wfull[mid].reshape(2 * w_rows, width),
        preferred_element_type=jnp.float32,
    )

    opposite_step(1)

    def project(t, d):
        at_pair = mid - 2 * t if d == 0 else mid + 2 * t - 1
        one = wrap(chip + at_pair - mid)
        left = heads[one]
        if d == 0:
            left = jnp.where(t == hops, jnp.zeros_like(left), left)
        both = jnp.concatenate([left, heads[wrap(one + 1)]], axis=1)
        hidden[...] += jnp.dot(
            both,
            wfull[pl.ds(at_pair, 2)].reshape(4 * w_rows, width),
            preferred_element_type=jnp.float32,
        )

    def project_step(t, carry):
        for d in range(2):
            w_shared(t, d).wait_recv()
            project(t, d)
        return carry

    lax.fori_loop(1, hops + 1, project_step, 0)

    state = hidden[...]
    hid_out[...] = state.astype(jnp.bfloat16)
    mean_square = jnp.mean(state * state, axis=-1, keepdims=True)
    normed = (
        state * lax.rsqrt(mean_square + 1e-06) * gain_ref[...].astype(jnp.float32).reshape(1, width)
    ).astype(jnp.bfloat16)
    for q in range(2):
        xown[q] = normed[q * half : (q + 1) * half]
    for q in range(2):
        for d in range(2):
            x_hop(d, q, 0).start()
    opposite_step(2)

    for r in others:
        gate_copy(r).wait_recv()
    lane = lax.broadcasted_iota(jnp.int32, (half, 128), 1)
    stacked = jnp.concatenate(
        [gates[r] for r in range(2 * reach + 1)]
        + [jnp.zeros((128 - 4 * (2 * reach + 1), tokens), jnp.float32)],
        axis=0,
    )
    gate_cols[...] = stacked.T
    for n, (_, _, theirs) in enumerate(weights):
        rcopy(theirs, theirs, ew_s.at[n], ew_r.at[n], sib).wait_recv()

    def served(x, places, halves, far):
        gu, down = (far_gu, far_d) if far else (wgu, wd)
        both = jnp.dot(x, gu[...], preferred_element_type=jnp.float32)
        parts = []
        for e in range(2):
            gate = []
            for d in range(2):
                at_rows = pl.ds(pl.multiple_of(halves[d] * half, half), half)
                column = 4 * places[d] + 2 * far + e
                gate.append(
                    jnp.sum(
                        jnp.where(lane == column, gate_cols[at_rows, :], 0.0),
                        axis=1,
                        keepdims=True,
                    )
                )
            gate = jnp.concatenate(gate, axis=0)
            v = both[:, e * ff : (e + 1) * ff]
            u = both[:, (2 + e) * ff : (3 + e) * ff]
            parts.append((v / (1.0 + jnp.exp(-v)) * u * gate).astype(jnp.bfloat16))
        return jnp.dot(
            jnp.concatenate(parts, axis=1), down[...], preferred_element_type=jnp.float32
        )

    def own_served(far):
        return served(xown[...].reshape(tokens, width), (reach, reach), (0, 1), far)

    def unit_served(u, far):
        h = u // 2 + 1
        last = u == 2 * (reach - 1)
        halves = [jnp.where(last, d, u % 2) for d in range(2)]
        return served(xbuf[u].reshape(tokens, width), (reach - h, reach + h), halves, far)

    def take_x(h):
        for q in range(2):
            for d in range(2):
                if h <= far_end(d, q):
                    x_hop(d, q, h - 1).wait_recv()
                if h < far_end(d, q):
                    x_hop(d, q, h).start()

    def natural(u, carry):
        contrib[u] = unit_served(u, 0)
        return carry

    def opposed(u, carry):
        contrib[u] += unit_served(u, 1)
        return carry

    def send_sum(d, q, h):
        u = unit(q, h)
        part = contrib[u, d * half : (d + 1) * half]
        if h < far_end(d, q):
            a_hop(d, q, h + 1).wait_recv()
            part = part + accbuf[u, d].astype(jnp.float32)
        accbuf[u, d] = part.astype(jnp.bfloat16)
        a_hop(d, q, h).start()

    own_part[...] = own_served(0)
    take_x(1)
    opposite_step(3)
    lax.fori_loop(0, 2, natural, 0)
    take_x(2)
    lax.fori_loop(2, 4, natural, 0)
    for n in range(4):
        for b in range(2):
            opposite(3, n, b, True).wait_recv()
    for copy in opposite_share(True):
        copy.start()
    take_x(3)
    lax.fori_loop(4, 6, natural, 0)
    for copy in opposite_share(False):
        copy.wait_recv()
    lax.fori_loop(4, 6, opposed, 0)
    send_sum(0, 1, 3)
    send_sum(1, 0, 3)
    take_x(4)
    lax.fori_loop(6, 7, natural, 0)
    lax.fori_loop(6, 7, opposed, 0)
    send_sum(0, 0, 4)
    send_sum(1, 1, 4)
    lax.fori_loop(2, 4, opposed, 0)
    send_sum(0, 1, 2)
    send_sum(1, 0, 2)
    send_sum(0, 0, 3)
    send_sum(1, 1, 3)
    lax.fori_loop(0, 2, opposed, 0)
    send_sum(0, 1, 1)
    send_sum(1, 0, 1)
    send_sum(0, 0, 2)
    send_sum(1, 1, 2)
    own_part[...] += own_served(1)
    send_sum(0, 0, 1)
    send_sum(1, 1, 1)
    for q in range(2):
        part = slice(q * half, (q + 1) * half)
        total = own_part[part]
        for d in (1 - q, q):
            a_hop(d, q, 1).wait_recv()
            total = total + home[d, q].astype(jnp.float32)
        mix_out[part] = total.astype(jnp.bfloat16)

    for part in range(2):
        for t in range(hops - 1):
            kv_hop(t, part).wait_send()

        @pl.when(core == 1)
        def _():
            kv_hop(hops - 1, part).wait_send()

    for t in range(hops):
        kv_shared(t).wait_send()

    @pl.when(me == 0)
    def _():
        for n in range(len(reached)):
            first_copy(n, sib).wait_send()

    @pl.when((core == 0) & (chip >= 4))
    def _():
        first_copy(1, sib).wait_send()

    @pl.when((core == 0) & (chip >= 5) & (chip % 2 == 1))
    def _():
        first_copy(0, sib).wait_send()

    def sent_z(h, carry):
        for d in range(2):
            for half_at in range(2):
                z_hop(d, h, half_at).wait_send()
        return carry

    lax.fori_loop(0, mid, sent_z, 0)

    def sent_plane(t, carry):
        each(lambda d, q: plane_copy(t, d, q).wait_send())

        @pl.when(t < hops)
        def _():
            each(lambda d, q: far_copy(t, d, q).wait_send())

        for d in range(2):
            w_share(t, d).wait_send()
        return carry

    lax.fori_loop(1, hops + 1, sent_plane, 0)
    own_share().wait_send()
    for d in range(2):
        for half_at in range(2):
            skip_copy(d, half_at).wait_send()

    for r in others:
        gate_copy(r).wait_send()
    for n in range(4):
        for second in (False, True):
            leg(n, second).wait_send()
        for stage in range(4):
            for b in range(2):
                opposite(stage, n, b).wait_send()
    for copy in opposite_share(True):
        copy.wait_send()
    for q in range(2):
        for d in range(2):
            for h in range(far_end(d, q)):
                x_hop(d, q, h).wait_send()
                a_hop(d, q, h + 1).wait_send()
    for n, (_, mine, _) in enumerate(weights):
        rcopy(mine, mine, ew_s.at[n], ew_r.at[n], sib).wait_send()


def shards(
    queries,
    token_key_heads,
    token_value_heads,
    residual,
    out_weight,
    norm_gain,
    w_gate,
    w_up,
    w_down,
    expert_ids,
    gate_weights,
    doc_of_block,
):
    blocks = lax.axis_size("seq")
    chips = blocks // 2
    tokens, width = residual.shape
    heads_width = queries.shape[1]
    kvw = token_key_heads.shape[1]
    ff = w_gate.shape[2]
    window = 8
    side = math.isqrt(lax.axis_size("pack"))
    hops = window // 2
    reach = chips // 4
    units = 2 * reach - 1
    group_rows = tokens * QUERY_HEADS // KEY_VALUE_HEADS
    half = tokens // 2
    vmem = pl.BlockSpec(memory_space=pltpu.VMEM)
    hbm = pl.BlockSpec(memory_space=pltpu.HBM)
    dma = pltpu.SemaphoreType.DMA
    bf16, f32 = jnp.bfloat16, jnp.float32
    return pl.pallas_call(
        functools.partial(slab_kernel, chips, side, window),
        out_shape=(
            jax.ShapeDtypeStruct((tokens, heads_width), bf16),
            jax.ShapeDtypeStruct((tokens, width), bf16),
            jax.ShapeDtypeStruct((tokens, width), bf16),
        ),
        in_specs=[pl.BlockSpec(memory_space=pltpu.SMEM)] + [hbm] * 5 + [vmem] + [hbm] * 5,
        out_specs=(vmem, vmem, vmem),
        scratch_shapes=[
            pltpu.VMEM((window + 2, tokens, 2 * kvw), bf16),
            pltpu.VMEM((KEY_VALUE_HEADS, group_rows, HEAD_SIZE), bf16),
            pltpu.VMEM((KEY_VALUE_HEADS, 1, group_rows), f32),
            pltpu.VMEM((KEY_VALUE_HEADS, 1, group_rows), f32),
            pltpu.VMEM((KEY_VALUE_HEADS, HEAD_SIZE, group_rows), f32),
            pltpu.VMEM((QUERY_HEADS, tokens, HEAD_SIZE), bf16),
            pltpu.VMEM((chips + 1, 2, out_weight.shape[0], width), bf16),
            pltpu.VMEM((tokens, width), bf16),
            pltpu.VMEM((TOP, tokens), jnp.int32),
            pltpu.VMEM((TOP, tokens), f32),
            pltpu.VMEM((tokens, width), f32),
            pltpu.VMEM((chips, 4, tokens), f32),
            pltpu.VMEM((2 * reach + 1, 4, tokens), f32),
            pltpu.VMEM((tokens, 128), f32),
            pltpu.VMEM((width, 4 * ff), bf16),
            pltpu.VMEM((2 * ff, width), bf16),
            pltpu.VMEM((width, 4 * ff), bf16),
            pltpu.VMEM((2 * ff, width), bf16),
            pltpu.VMEM((2, width // side**2, ff), bf16),
            pltpu.VMEM((2, ff // (2 * side), width // side), bf16),
            pltpu.VMEM((2, half, width), bf16),
            pltpu.VMEM((units, 2, half, width), bf16),
            pltpu.VMEM((units, 2, half, width), bf16),
            pltpu.VMEM((2, 2, half, width), bf16),
            pltpu.VMEM((units, tokens, width), f32),
            pltpu.VMEM((tokens, width), f32),
            dma((6 + QUERY_HEADS,)),
            dma((hops, 2)),
            dma((hops, 2)),
            dma((hops,)),
            dma((hops,)),
            dma((8,)),
            dma,
            dma((2, chips // 2, 2)),
            dma((2, chips // 2, 2)),
            dma((hops, 2, 4)),
            dma((hops, 2, 4)),
            dma((hops, 2, 4)),
            dma((hops, 2, 4)),
            dma((hops + 1, 2)),
            dma((hops + 1, 2)),
            dma((2 * reach + 1,)),
            dma((2 * reach + 1,)),
            dma((3,)),
            dma((3,)),
            dma((3,)),
            dma((2, 4)),
            dma((2, 4)),
            dma((4, 4, 2)),
            dma((4, 4, 2)),
            dma((3,)),
            dma((3,)),
            dma((units, 2)),
            dma((units, 2)),
            dma((units, 2)),
            dma((units, 2)),
            dma((2, 2)),
            dma((2, 2)),
        ],
        compiler_params=pltpu.CompilerParams(
            collective_id=0, has_side_effects=True, vmem_limit_bytes=48 << 20
        ),
    )(
        doc_of_block,
        *(pltpu.with_memory_space_constraint(a, pltpu.HBM) for a in (queries, token_key_heads, token_value_heads, residual, out_weight)),
        norm_gain,
        *(pltpu.with_memory_space_constraint(a, pltpu.HBM) for a in (expert_ids.T, gate_weights.T, w_gate, w_up, w_down)),
    )


def solution(mesh):
    in_specs = (
        P(("pack", "seq"), None),
        P(("pack", "seq"), None),
        P(("pack", "seq"), None),
        P(("pack", "seq"), None),
        P("seq", None),
        P(),
        P("seq", None, None),
        P("seq", None, None),
        P("seq", None, None),
        P(("pack", "seq"), None),
        P(("pack", "seq"), None),
        P("pack"),
    )
    out_specs = (P(("pack", "seq"), None), P(("pack", "seq"), None), P(("pack", "seq"), None))
    return jax.shard_map(shards, mesh=mesh, in_specs=in_specs, out_specs=out_specs, check_vma=False)
```
